128 devices in a mesh: dp: 8 (over x_hi, z), expert: 16 (over y, x_lo, core).
Axes of the slice: x: 4 (x_hi: 2, x_lo: 2; x = x_hi * 2 + x_lo), y: 4, z: 4, core: 2. Of those that a mesh axis runs over, the one named last changes fastest.
Arguments:
- tokens: bfloat16 [32768, 2048], P(('dp', 'expert')), may hold values from -6 to 6
- expert_ids: int32 [32768, 4], P(('dp', 'expert')), may hold values from 0 to 15, as said below
- gates: float32 [32768, 4], P(('dp', 'expert')), may hold values from 0.1 to 1
- w_gate: bfloat16 [16, 2048, 384], P('expert'), may hold values from -0.125 to 0.125
- w_up: bfloat16 [16, 2048, 384], P('expert'), may hold values from -0.125 to 0.125
- w_down: bfloat16 [16, 2048, 384], P('expert'), may hold values from -0.3125 to 0.3125
- cotangent: bfloat16 [32768, 2048], P(('dp', 'expert')), may hold values from -6 to 6
Outputs:
- mixed: bfloat16 [32768, 2048], P(('dp', 'expert'))
- tokens_grad: bfloat16 [32768, 2048], P(('dp', 'expert'))
- gates_grad: float32 [32768, 4], P(('dp', 'expert'))
- gate_grad: float32 [16, 2048, 384], P('expert', 'dp')
- up_grad: float32 [16, 2048, 384], P('expert', 'dp')
- down_grad: float32 [16, 2048, 384], P('expert', 'dp')
The draws below stay inside these ranges and needn't reach their ends.
Inputs may be any that keep to these rules, and one draw needn't show every extreme that they name: `expert_ids`: each row holds 4 different experts. One expert, the same in every draw position, is named by every token. Among the 256 tokens of one device every other expert is named at most 52 times, and one of them is named exactly 52 times on every device.
All inputs are finite; a program needn't handle non-finite values.
Results may differ from the reference program's by a relative error of at most 0.014.
Values may be sent and summed in bfloat16 or wider, within the bound.
A program may use at most 128 MiB of HBM per device.

```python
import math
import jax
import jax.numpy as jnp
from jax import lax

D = 2048
FF = 384
TOPK = 4
TOK_DEV = 256
EXPERTS = 16
TOKENS = 32768


def draw_expert_ids(key, part):
    cold_count = EXPERTS - 1
    spread = TOK_DEV * (TOPK - 1)
    surplus = max(spread % cold_count, 1)
    hot_id = jax.random.randint(jax.random.fold_in(key, 101), (), 0, EXPERTS).astype(jnp.int32)
    base_id = jax.random.randint(jax.random.fold_in(key, 102), (), 0, cold_count).astype(jnp.int32)
    block_keys = jax.random.split(jax.random.fold_in(key, 103), TOKENS // TOK_DEV)

    def one_block(block_key):
        perm_key, shift_key, order_key = jax.random.split(block_key, 3)
        ranking = jax.random.permutation(perm_key, TOK_DEV).astype(jnp.int32)
        offset = base_id - jax.random.randint(shift_key, (), 0, surplus).astype(jnp.int32)
        slot_index = ranking[:, None] * (TOPK - 1) + jnp.arange(TOPK - 1, dtype=jnp.int32)[None, :]
        cold_ids = (slot_index + offset) % cold_count
        cold_ids = cold_ids + (cold_ids >= hot_id).astype(jnp.int32)
        chosen = jnp.concatenate([jnp.full((TOK_DEV, 1), hot_id, jnp.int32), cold_ids.astype(jnp.int32)], axis=1)
        scores = jax.random.randint(order_key, (TOK_DEV, TOPK), 0, 1 << 20).astype(jnp.int32) * TOPK + jnp.arange(TOPK, dtype=jnp.int32)[None, :]
        ordering = jnp.argsort(scores, axis=1)
        return jnp.take_along_axis(chosen, ordering, axis=1)
    return lax.map(one_block, block_keys).reshape(TOKENS, TOPK).astype(jnp.int32)


def levels(key, shape, shards, least, top_value):
    factor_of = 1.0
    for axis_at, shards_of in shards:
        heights = jax.random.uniform(jax.random.fold_in(jax.random.fold_in(key, 6), axis_at), (shards_of,), jnp.float32, least / len(shards), top_value / len(shards))
        factor_of = factor_of * jnp.repeat(jnp.exp(heights), shape[axis_at] // shards_of).reshape((-1,) + (1,) * (len(shape) - 1 - axis_at))
    return factor_of


def noise(own_key, dims, deviation, limit, pieces=(), held_as=jnp.bfloat16):
    array = jax.random.normal(own_key, dims, jnp.float32) * deviation
    if len(pieces) > 0:
        array = levels(own_key, dims, pieces, -0.22, 0.18) * array
    return jnp.clip(array, min=-limit, max=limit).astype(held_as)


def setup_inputs(seed: int = 0) -> dict:
    arg_keys = jax.random.split(jax.random.key(seed), 8)
    return {
        "tokens": noise(arg_keys[0], (TOKENS, D), 1.0, 6.0, ((0, 128),)),
        "expert_ids": draw_expert_ids(jax.random.fold_in(arg_keys[7], 71), 0),
        "gates": jnp.clip(jnp.exp(math.log(1.0) - 2.3025851 * jax.random.uniform(arg_keys[2], (TOKENS, TOPK), jnp.float32) ** levels(arg_keys[2], (TOKENS, TOPK), ((0, 128),), -0.2, 0.2)), 0.1, 1.0),
        "w_gate": noise(arg_keys[3], (EXPERTS, D, FF), D ** -0.5, 0.125, ((0, 16),)),
        "w_up": noise(arg_keys[4], (EXPERTS, D, FF), D ** -0.5, 0.125, ((0, 16),)),
        "w_down": noise(arg_keys[5], (EXPERTS, D, FF), FF ** -0.5, 0.3125, ((0, 16),)),
        "cotangent": noise(arg_keys[6], (TOKENS, D), 1.0, 6.0, ((0, 128),)),
    }


def expert_forward(rows, weight_gate, weight_up, weight_down):
    gate_act = jnp.dot(rows, weight_gate, preferred_element_type=jnp.float32)
    up_act = jnp.dot(rows, weight_up, preferred_element_type=jnp.float32)
    hidden = (jax.nn.silu(gate_act) * up_act).astype(jnp.bfloat16)
    output = lax.dot_general(hidden, weight_down, (((1,), (1,)), ((), ())), preferred_element_type=jnp.float32).astype(jnp.bfloat16)
    return gate_act, up_act, hidden, output


def expert_backward(rows, upstream, weight_gate, weight_up, weight_down, gate_act, up_act, hidden):
    hidden_grad = jnp.dot(upstream, weight_down, preferred_element_type=jnp.float32)
    sigma = jax.nn.sigmoid(gate_act)
    gate_pre = (hidden_grad * up_act * sigma * (1.0 + gate_act * (1.0 - sigma))).astype(jnp.bfloat16)
    up_pre = (hidden_grad * gate_act * sigma).astype(jnp.bfloat16)
    contract = (((1,), (1,)), ((), ()))
    input_part = (lax.dot_general(gate_pre, weight_gate, contract, preferred_element_type=jnp.float32)
                  + lax.dot_general(up_pre, weight_up, contract, preferred_element_type=jnp.float32)).astype(jnp.bfloat16)
    over_rows = (((0,), (0,)), ((), ()))
    grad_gate = lax.dot_general(rows, gate_pre, over_rows, preferred_element_type=jnp.float32)
    grad_upper = lax.dot_general(rows, up_pre, over_rows, preferred_element_type=jnp.float32)
    grad_down = lax.dot_general(upstream, hidden, over_rows, preferred_element_type=jnp.float32)
    return input_part, grad_gate, grad_upper, grad_down


def reference(tokens, expert_ids, gates, w_gate, w_up, w_down, cotangent):
    rows_all = TOKENS * TOPK
    block = min(512, rows_all)
    flat_ids = expert_ids.reshape(-1)
    ordering = jnp.argsort(flat_ids, stable=True).astype(jnp.int32)
    sorted_ids = flat_ids[ordering]
    sorted_gates = gates.reshape(-1)[ordering]
    block_count = rows_all // block

    def one_block(carry, block_index):
        mixed, tokens_grad, grad_g, grad_u, grad_d = carry
        start = (block_index * block).astype(jnp.int32)
        picked = lax.dynamic_slice_in_dim(ordering, start, block)
        ids_here = lax.dynamic_slice_in_dim(sorted_ids, start, block)
        gate_here = lax.dynamic_slice_in_dim(sorted_gates, start, block)
        token_index = (picked // TOPK).astype(jnp.int32)
        rows = tokens[token_index]
        upstream = cotangent[token_index]
        slot_grad = (gate_here[:, None] * upstream.astype(jnp.float32)).astype(jnp.bfloat16)

        def per_expert(expert, inner):
            out_sum, input_sum, grad_g, grad_u, grad_d = inner
            selected = (ids_here == expert)[:, None]
            xin = jnp.where(selected, rows, jnp.zeros_like(rows))
            din = jnp.where(selected, slot_grad, jnp.zeros_like(slot_grad))
            weight_gate = lax.dynamic_index_in_dim(w_gate, expert, 0, keepdims=False)
            weight_up = lax.dynamic_index_in_dim(w_up, expert, 0, keepdims=False)
            weight_down = lax.dynamic_index_in_dim(w_down, expert, 0, keepdims=False)
            gate_act, up_act, hidden, output = expert_forward(xin, weight_gate, weight_up, weight_down)
            input_part, grad_gate, grad_upper, grad_down = expert_backward(xin, din, weight_gate, weight_up, weight_down, gate_act, up_act, hidden)
            out_sum = out_sum + output.astype(jnp.float32)
            input_sum = input_sum + input_part.astype(jnp.float32)
            grad_g = grad_g.at[expert].add(grad_gate)
            grad_u = grad_u.at[expert].add(grad_upper)
            grad_d = grad_d.at[expert].add(grad_down)
            return out_sum, input_sum, grad_g, grad_u, grad_d

        zero_rows = jnp.zeros((block, D), jnp.float32)
        out_sum, input_sum, grad_g, grad_u, grad_d = lax.fori_loop(
            ids_here[0], ids_here[block - 1] + 1, per_expert, (zero_rows, zero_rows, grad_g, grad_u, grad_d))
        dgate_here = jnp.sum(upstream.astype(jnp.float32) * out_sum, axis=1)
        mixed = mixed.at[token_index].add(gate_here[:, None] * out_sum)
        tokens_grad = tokens_grad.at[token_index].add(input_sum)
        return (mixed, tokens_grad, grad_g, grad_u, grad_d), dgate_here

    zero_tokens = jnp.zeros((TOKENS, D), jnp.float32)
    zero_weights = jnp.zeros((EXPERTS, D, FF), jnp.float32)
    final, dgates_sorted = lax.scan(one_block, (zero_tokens, zero_tokens, zero_weights, zero_weights, zero_weights),
                                    jnp.arange(block_count, dtype=jnp.int32))
    mixed, tokens_grad, grad_g, grad_u, grad_d = final
    gates_grad = jnp.zeros((rows_all,), jnp.float32).at[ordering].set(dgates_sorted.reshape(-1)).reshape(TOKENS, TOPK)
    return (mixed.astype(jnp.bfloat16), tokens_grad.astype(jnp.bfloat16), gates_grad, grad_g, grad_u, grad_d)
```

```python
import functools

import jax
import jax.numpy as jnp
from jax import lax
from jax.experimental import pallas as pl
from jax.experimental.pallas import tpu as pltpu
from jax.sharding import PartitionSpec as P

D = 2048
FF = 384
TOPK = 4
MESH = pl.DeviceIdType.MESH
ROW_TILE = 8


def exchange_kernel(experts, a_ref, b_ref, ra_ref, rb_ref, own, send_sem, recv_sem, own_sem):
    me = lax.axis_index("expert")
    group = lax.axis_index("dp")
    barrier = pltpu.get_barrier_semaphore()
    for step in range(1, experts):
        peer = (me + step) % experts
        pl.semaphore_signal(barrier, inc=1, device_id=(group, peer), device_id_type=MESH)
    pl.semaphore_wait(barrier, experts - 1)
    copies = []
    for which, (src, dst) in enumerate(((a_ref, ra_ref), (b_ref, rb_ref))):
        for step in range(1, experts):
            peer = (me + step) % experts
            copy = pltpu.make_async_remote_copy(
                src_ref=src.at[peer],
                dst_ref=dst.at[me],
                send_sem=send_sem.at[which, step],
                recv_sem=recv_sem.at[which, step],
                device_id=(group, peer),
                device_id_type=MESH,
            )
            copy.start()
            copies.append(copy)
    for which, (src, dst) in enumerate(((a_ref, ra_ref), (b_ref, rb_ref))):
        load = pltpu.make_async_copy(src.at[me], own.at[which], own_sem.at[which])
        load.start()
        load.wait()
        store = pltpu.make_async_copy(own.at[which], dst.at[me], own_sem.at[which])
        store.start()
        store.wait()
    for copy in copies:
        copy.wait()


def exchange(a, b, collective_id, name):
    experts = a.shape[0]
    shape = jax.ShapeDtypeStruct(a.shape, a.dtype)
    return pl.pallas_call(
        functools.partial(exchange_kernel, experts),
        out_shape=(shape, shape),
        in_specs=[pl.BlockSpec(memory_space=pltpu.HBM)] * 2,
        out_specs=(pl.BlockSpec(memory_space=pltpu.HBM),) * 2,
        scratch_shapes=[
            pltpu.VMEM((2,) + a.shape[1:], a.dtype),
            pltpu.SemaphoreType.DMA((2, experts)),
            pltpu.SemaphoreType.DMA((2, experts)),
            pltpu.SemaphoreType.DMA((2,)),
        ],
        compiler_params=pltpu.CompilerParams(collective_id=collective_id, has_side_effects=True),
        cost_estimate=pl.CostEstimate(flops=0, bytes_accessed=200_000_000, transcendentals=0),
        name=name,
    )(a, b)


def expert_forward(rows, weight_gate, weight_up, weight_down):
    gate_act = jnp.dot(rows, weight_gate, preferred_element_type=jnp.float32)
    up_act = jnp.dot(rows, weight_up, preferred_element_type=jnp.float32)
    hidden = (jax.nn.silu(gate_act) * up_act).astype(jnp.bfloat16)
    output = lax.dot_general(
        hidden, weight_down, (((1,), (1,)), ((), ())), preferred_element_type=jnp.float32
    ).astype(jnp.bfloat16)
    return (gate_act, up_act, hidden, output)


def expert_backward(rows, upstream, weight_gate, weight_up, weight_down, gate_act, up_act, hidden):
    hidden_grad = jnp.dot(upstream, weight_down, preferred_element_type=jnp.float32)
    sigma = jax.nn.sigmoid(gate_act)
    gate_pre = (hidden_grad * up_act * sigma * (1.0 + gate_act * (1.0 - sigma))).astype(
        jnp.bfloat16
    )
    up_pre = (hidden_grad * gate_act * sigma).astype(jnp.bfloat16)
    contract = (((1,), (1,)), ((), ()))
    input_part = (
        lax.dot_general(gate_pre, weight_gate, contract, preferred_element_type=jnp.float32)
        + lax.dot_general(up_pre, weight_up, contract, preferred_element_type=jnp.float32)
    ).astype(jnp.bfloat16)
    over_rows = (((0,), (0,)), ((), ()))
    grad_gate = lax.dot_general(rows, gate_pre, over_rows, preferred_element_type=jnp.float32)
    grad_upper = lax.dot_general(rows, up_pre, over_rows, preferred_element_type=jnp.float32)
    grad_down = lax.dot_general(upstream, hidden, over_rows, preferred_element_type=jnp.float32)
    return (input_part, grad_gate, grad_upper, grad_down)


def per_device(tokens, expert_ids, gates, w_gate, w_up, w_down, cotangent):
    experts = lax.axis_size("expert")
    groups = lax.axis_size("dp")
    tok_rows = tokens.shape[0]
    capacity = (tok_rows * (TOPK - 1) + experts - 2) // (experts - 1)
    capacity = (capacity + ROW_TILE - 1) // ROW_TILE * ROW_TILE
    over_rows = (((0,), (0,)), ((), ()))
    highest = lax.Precision.HIGHEST
    expert_range = jnp.arange(experts, dtype=jnp.int32)
    matches = (expert_ids[:, :, None] == expert_range).astype(jnp.int32)
    counts = jnp.sum(matches, axis=(0, 1))
    hot_expert = jnp.argmax(counts)
    is_hot = expert_ids == hot_expert
    is_owner = lax.axis_index("expert") == hot_expert
    own_weights = (w_gate[0], w_up[0], w_down[0])

    piece = D // groups
    start = lax.axis_index("dp") * piece
    own_piece = jnp.stack(
        [lax.dynamic_slice_in_dim(weight, start, piece, 0) for weight in own_weights]
    )
    hot_piece = lax.psum(jnp.where(is_owner, own_piece, 0).astype(jnp.bfloat16), "expert")
    shadow_all = lax.all_gather(hot_piece, "dp", axis=1, tiled=True)
    shadow = (shadow_all[0], shadow_all[1], shadow_all[2])

    flat_matches = matches.reshape(tok_rows * TOPK, experts)
    before = jnp.cumsum(flat_matches, axis=0) - flat_matches
    position = jnp.sum(before * flat_matches, axis=1)
    target = jnp.where(is_hot.reshape(-1), -1, expert_ids.reshape(-1) * capacity + position)
    slot_ids = jnp.arange(experts * capacity, dtype=jnp.int32)
    dispatch_f = (slot_ids[:, None] == target[None, :]).astype(jnp.float32)
    per_token_f = jnp.sum(dispatch_f.reshape(experts * capacity, tok_rows, TOPK), axis=2)
    per_token = per_token_f.astype(jnp.bfloat16)
    slot_gate = jnp.dot(
        dispatch_f, gates.reshape(-1), precision=highest, preferred_element_type=jnp.float32
    )
    outgoing = jnp.dot(per_token, tokens, preferred_element_type=jnp.float32).astype(jnp.bfloat16)
    copied = jnp.dot(per_token, cotangent, preferred_element_type=jnp.float32)
    outgoing_grad = (slot_gate[:, None] * copied).astype(jnp.bfloat16)
    rows, incoming_grad = exchange(
        outgoing.reshape(experts, capacity, D),
        outgoing_grad.reshape(experts, capacity, D),
        1,
        "dispatch",
    )
    rows = rows.reshape(-1, D)
    incoming_grad = incoming_grad.reshape(-1, D)
    gate_act, up_act, hidden, expert_out = expert_forward(rows, *own_weights)
    input_rows, own_gate, own_upper, own_down = expert_backward(
        rows, incoming_grad, *own_weights, gate_act, up_act, hidden
    )
    hot_gate, hot_up, hot_hidden, hot_out = expert_forward(tokens, *shadow)
    upstream = cotangent.astype(jnp.float32)
    hot_weight = jnp.sum(jnp.where(is_hot, gates, 0.0), axis=1)
    hot_upstream = (hot_weight[:, None] * upstream).astype(jnp.bfloat16)
    hot_input, hot_gate_grad, hot_upper_grad, hot_down_grad = expert_backward(
        tokens, hot_upstream, *shadow, hot_gate, hot_up, hot_hidden
    )
    parts = jnp.stack(
        [own_gate, own_upper, own_down, hot_gate_grad, hot_upper_grad, hot_down_grad]
    ).astype(jnp.bfloat16)
    sums = lax.psum_scatter(parts, "dp", scatter_dimension=1, tiled=True)
    hot_total = lax.psum(sums[3:].astype(jnp.float32), "expert")
    grads = sums[:3].astype(jnp.float32) + jnp.where(is_owner, hot_total, 0.0)

    returned, back_rows = exchange(
        expert_out.reshape(experts, capacity, D),
        input_rows.reshape(experts, capacity, D),
        2,
        "combine",
    )
    returned_f = returned.reshape(-1, D).astype(jnp.float32)
    hot_out_f = hot_out.astype(jnp.float32)
    weighted = slot_gate[:, None] * returned_f
    mixed_cold = lax.dot_general(
        per_token_f, weighted, over_rows, precision=highest, preferred_element_type=jnp.float32
    )
    mixed = (mixed_cold + hot_weight[:, None] * hot_out_f).astype(jnp.bfloat16)
    slot_dot = jnp.sum(returned_f * copied, axis=1)
    cold_gates = jnp.dot(
        slot_dot, dispatch_f, precision=highest, preferred_element_type=jnp.float32
    ).reshape(tok_rows, TOPK)
    hot_dot = jnp.sum(upstream * hot_out_f, axis=1)
    gates_grad = cold_gates + jnp.where(is_hot, hot_dot[:, None], 0.0)
    cold_input = lax.dot_general(
        per_token, back_rows.reshape(-1, D), over_rows, preferred_element_type=jnp.float32
    )
    tokens_grad = (cold_input + hot_input.astype(jnp.float32)).astype(jnp.bfloat16)
    return (mixed, tokens_grad, gates_grad, grads[0][None], grads[1][None], grads[2][None])


def solution(mesh):
    return jax.shard_map(
        per_device,
        mesh=mesh,
        in_specs=(
            P(("dp", "expert"), None),
            P(("dp", "expert"), None),
            P(("dp", "expert"), None),
            P("expert", None, None),
            P("expert", None, None),
            P("expert", None, None),
            P(("dp", "expert"), None),
        ),
        out_specs=(
            P(("dp", "expert"), None),
            P(("dp", "expert"), None),
            P(("dp", "expert"), None),
            P("expert", "dp", None),
            P("expert", "dp", None),
            P("expert", "dp", None),
        ),
        check_vma=False,
    )
```

```python
import functools

import jax
import jax.numpy as jnp
from jax import lax
from jax.experimental import pallas as pl
from jax.experimental.pallas import tpu as pltpu
from jax.sharding import PartitionSpec as P

D = 2048
FF = 384
TOPK = 4
MESH = pl.DeviceIdType.MESH
ROW_TILE = 8
BF16 = jnp.bfloat16
F32 = jnp.float32


class Place:
    def __init__(self):
        self.g = lax.axis_index("dp")
        self.e = lax.axis_index("expert")
        self.xh, self.z = self.g // 4, self.g % 4
        self.q, self.c = self.e // 2, self.e % 2
        self.y, self.xl = self.q // 2, self.q % 2

    def chip(self, step):
        return (self.g, ((self.q + step) % 8) * 2 + self.c)

    def plane(self, dy, dx, dc):
        return ((self.y + dy) % 4) * 4 + ((self.xl + dx) % 2) * 2 + (self.c + dc) % 2

    def partner(self):
        return (self.g, self.q * 2 + 1 - self.c)

    def along_z(self, step):
        return (self.xh * 4 + (self.z + step) % 4, self.e)

    def across(self):
        return ((1 - self.xh) * 4 + self.z, self.e)


class Copies:
    def __init__(self, send_sem, recv_sem):
        self.send_sem, self.recv_sem = send_sem, recv_sem
        self.started = []

    def send(self, src, dst, device):
        at = len(self.started)
        copy = pltpu.make_async_remote_copy(
            src_ref=src,
            dst_ref=dst,
            send_sem=self.send_sem.at[at],
            recv_sem=self.recv_sem.at[at],
            device_id=device,
            device_id_type=MESH,
        )
        copy.start()
        self.started.append(copy)
        return copy

    def finish(self):
        for copy in self.started:
            copy.wait_send()


COLUMN = [(dy, 0, dc) for dy in (1, 3, 2) for dc in (0, 1)] + [(0, 0, 1)]
BESIDE = [(dy, 1, dc) for dy in (0, 1, 3, 2) for dc in (0, 1)]


def enter(place):
    barrier = pltpu.get_barrier_semaphore()
    peers = [(place.g, place.plane(*step)) for step in COLUMN + BESIDE]
    peers += [place.along_z(step) for step in (1, 3, 2)] + [place.across()]
    for peer in peers:
        pl.semaphore_signal(barrier, inc=1, device_id=peer, device_id_type=MESH)
    pl.semaphore_wait(barrier, len(peers))


def send_blocks(place, copies, src, dst, steps):
    sent = []
    for step in steps:
        peer = place.plane(*step)
        sent.append(copies.send(src.at[peer], dst.at[place.e], (place.g, peer)))
    return sent


def move_own(place, src, dst, stage, sem):
    load = pltpu.make_async_copy(src.at[place.e], stage, sem)
    load.start()
    load.wait()
    store = pltpu.make_async_copy(stage, dst.at[place.e], sem)
    store.start()
    store.wait()


def dispatch_kernel(
    hot_ref, a_ref, b_ref, piece_ref, ra_ref, rb_ref, hw_ref,
    stage, cand, chosen, landed, mine, send_sem, recv_sem, own_sem,
):
    place = Place()
    g, q, c = place.g, place.q, place.c
    enter(place)
    copies = Copies(send_sem, recv_sem)
    hot = hot_ref[0]
    swap = copies.send(piece_ref.at[:, 1 - c], cand.at[c], place.partner())
    local = pltpu.make_async_copy(piece_ref.at[:, c], cand.at[c], own_sem.at[0])
    local.start()
    local.wait()
    swap.wait_recv()
    chosen[...] = cand[hot % 2]
    scatter = [
        copies.send(chosen.at[:, (q + k) % 8], landed.at[q], place.chip(k)) for k in range(1, 8)
    ]
    landed[q] = chosen[:, q]
    for copy in scatter:
        copy.wait_recv()
    mine[...] = landed[hot // 2]
    gather = [
        copies.send(mine, hw_ref.at[:, g, c, q], place.chip(k)) for k in range(1, 8)
    ]
    local = pltpu.make_async_copy(mine, hw_ref.at[:, g, c, q], own_sem.at[0])
    local.start()
    blocks = send_blocks(place, copies, a_ref, ra_ref, COLUMN)
    local.wait()
    for copy in gather:
        copy.wait_recv()
    across = copies.send(hw_ref.at[:, g, c], hw_ref.at[:, g, c], place.across())
    first = [
        copies.send(hw_ref.at[:, g, c], hw_ref.at[:, g, c], place.along_z(k)) for k in (1, 3, 2)
    ]
    blocks += send_blocks(place, copies, a_ref, ra_ref, BESIDE)
    blocks += send_blocks(place, copies, b_ref, rb_ref, BESIDE + COLUMN)
    across.wait_recv()
    other = (1 - place.xh) * 4 + place.z
    first += [
        copies.send(hw_ref.at[:, other, c], hw_ref.at[:, other, c], place.along_z(k))
        for k in (1, 3, 2)
    ]
    move_own(place, a_ref, ra_ref, stage, own_sem.at[0])
    move_own(place, b_ref, rb_ref, stage, own_sem.at[0])
    for copy in first:
        copy.wait_recv()
    last = copies.send(hw_ref.at[:, :, c], hw_ref.at[:, :, c], place.partner())
    last.wait_recv()
    for copy in blocks:
        copy.wait_recv()
    copies.finish()


def dispatch(hot_expert, a, b, piece):
    block = jax.ShapeDtypeStruct(a.shape, a.dtype)
    return pl.pallas_call(
        dispatch_kernel,
        out_shape=(block, block, jax.ShapeDtypeStruct((3, 8, 2, 8, 16, FF), BF16)),
        in_specs=[pl.BlockSpec(memory_space=pltpu.SMEM)]
        + [pl.BlockSpec(memory_space=pltpu.HBM)] * 3,
        out_specs=(pl.BlockSpec(memory_space=pltpu.HBM),) * 3,
        scratch_shapes=[
            pltpu.VMEM(a.shape[1:], BF16),
            pltpu.VMEM((2, 3, 8, 16, FF), BF16),
            pltpu.VMEM((3, 8, 16, FF), BF16),
            pltpu.VMEM((8, 3, 16, FF), BF16),
            pltpu.VMEM((3, 16, FF), BF16),
            pltpu.SemaphoreType.DMA((64,)),
            pltpu.SemaphoreType.DMA((64,)),
            pltpu.SemaphoreType.DMA((1,)),
        ],
        compiler_params=pltpu.CompilerParams(collective_id=1, has_side_effects=True),
        cost_estimate=pl.CostEstimate(flops=0, bytes_accessed=200_000_000, transcendentals=0),
        name="dispatch",
    )(hot_expert.reshape(1), a, b, piece)


def combine_kernel(
    c_ref, d_ref, own_ref, hot_ref, rc_ref, rd_ref, sum_ref, tot_ref,
    stage, half, half_in, hz_in, hz_out, hx_in, hp, h_in, h_mine, tot,
    quarter, g_in, g_out, gx_in, send_sem, recv_sem, own_sem,
):
    place = Place()
    g, q, c, z, xh = place.g, place.q, place.c, place.z, place.xh
    enter(place)
    copies = Copies(send_sem, recv_sem)
    swap = copies.send(hot_ref.at[:, :, :, 1 - c], half_in, place.partner())
    local_h = pltpu.make_async_copy(hot_ref.at[:, :, :, c], half, own_sem.at[0])
    local_h.start()
    local_g = pltpu.make_async_copy(own_ref.at[:, :, z], quarter, own_sem.at[1])
    local_g.start()
    blocks = send_blocks(place, copies, c_ref, rc_ref, BESIDE + COLUMN)
    local_h.wait()
    swap.wait_recv()

    @pl.loop(0, 24)
    def _(i):
        w, gg = i // 8, i % 8
        at = (w, gg // 4, gg % 4)
        half[at] = (half[at].astype(F32) + half_in[at].astype(F32)).astype(BF16)

    hz = [
        copies.send(half.at[:, :, (z + k) % 4], hz_in.at[n], place.along_z(k))
        for n, k in enumerate((1, 3, 2))
    ]
    gz = [
        copies.send(own_ref.at[:, :, (z + k) % 4], g_in.at[n], place.along_z(k))
        for n, k in enumerate((1, 3, 2))
    ]
    blocks += send_blocks(place, copies, d_ref, rd_ref, COLUMN)
    for copy in hz:
        copy.wait_recv()

    @pl.loop(0, 6)
    def _(i):
        at = (i // 2, i % 2)
        total = half[at[0], at[1], z].astype(F32)
        for n in range(3):
            total += hz_in[(n,) + at].astype(F32)
        hz_out[at] = total.astype(BF16)

    hx = copies.send(hz_out.at[:, 1 - xh], hx_in, place.across())
    blocks += send_blocks(place, copies, d_ref, rd_ref, BESIDE)
    move_own(place, c_ref, rc_ref, stage, own_sem.at[0])
    move_own(place, d_ref, rd_ref, stage, own_sem.at[0])
    hx.wait_recv()
    hp[...] = (hz_out[:, xh].astype(F32) + hx_in[...].astype(F32)).astype(BF16)
    scatter = [
        copies.send(hp.at[:, (q + k) % 8], h_in.at[q], place.chip(k)) for k in range(1, 8)
    ]
    h_in[q] = hp[:, q]
    local_g.wait()
    for copy in gz:
        copy.wait_recv()

    @pl.loop(0, 6)
    def _(i):
        at = (i // 2, i % 2)
        total = quarter[at].astype(F32)
        for n in range(3):
            total += g_in[(n,) + at].astype(F32)
        g_out[at] = total

    @pl.loop(0, 3)
    def _(w):
        quarter[w, 1 - xh] = g_out[w, 1 - xh].astype(BF16)

    gx = copies.send(quarter.at[:, 1 - xh], gx_in, place.across())
    for copy in scatter:
        copy.wait_recv()
    total = h_in[0].astype(F32)
    for n in range(1, 8):
        total += h_in[n].astype(F32)
    h_mine[...] = total.astype(BF16)
    gather = [copies.send(h_mine, tot.at[:, c, q], place.chip(k)) for k in range(1, 8)]
    tot[:, c, q] = h_mine[...]
    for copy in gather:
        copy.wait_recv()
    last = copies.send(tot.at[:, c], tot.at[:, c], place.partner())
    gx.wait_recv()

    @pl.loop(0, 3)
    def _(w):
        g_out[w, xh] = g_out[w, xh] + gx_in[w].astype(F32)

    store = pltpu.make_async_copy(g_out.at[:, xh], sum_ref, own_sem.at[0])
    store.start()
    store.wait()
    last.wait_recv()
    store = pltpu.make_async_copy(tot, tot_ref, own_sem.at[0])
    store.start()
    store.wait()
    for copy in blocks:
        copy.wait_recv()
    copies.finish()


def combine(c, d, own, hot):
    block = jax.ShapeDtypeStruct(c.shape, c.dtype)
    return pl.pallas_call(
        combine_kernel,
        out_shape=(
            block,
            block,
            jax.ShapeDtypeStruct((3, 256, FF), F32),
            jax.ShapeDtypeStruct((3, 2, 8, 16, FF), BF16),
        ),
        in_specs=[pl.BlockSpec(memory_space=pltpu.HBM)] * 4,
        out_specs=(pl.BlockSpec(memory_space=pltpu.HBM),) * 4,
        scratch_shapes=[
            pltpu.VMEM(c.shape[1:], BF16),
            pltpu.VMEM((3, 2, 4, 8, 16, FF), BF16),
            pltpu.VMEM((3, 2, 4, 8, 16, FF), BF16),
            pltpu.VMEM((3, 3, 2, 8, 16, FF), BF16),
            pltpu.VMEM((3, 2, 8, 16, FF), BF16),
            pltpu.VMEM((3, 8, 16, FF), BF16),
            pltpu.VMEM((3, 8, 16, FF), BF16),
            pltpu.VMEM((8, 3, 16, FF), BF16),
            pltpu.VMEM((3, 16, FF), BF16),
            pltpu.VMEM((3, 2, 8, 16, FF), BF16),
            pltpu.VMEM((3, 2, 256, FF), BF16),
            pltpu.VMEM((3, 3, 2, 256, FF), BF16),
            pltpu.VMEM((3, 2, 256, FF), F32),
            pltpu.VMEM((3, 256, FF), BF16),
            pltpu.SemaphoreType.DMA((64,)),
            pltpu.SemaphoreType.DMA((64,)),
            pltpu.SemaphoreType.DMA((2,)),
        ],
        compiler_params=pltpu.CompilerParams(
            collective_id=2, has_side_effects=True, vmem_limit_bytes=48 << 20
        ),
        cost_estimate=pl.CostEstimate(flops=0, bytes_accessed=200_000_000, transcendentals=0),
        name="combine",
    )(c, d, own.reshape(3, 2, 4, 256, FF), hot.reshape(3, 2, 4, 2, 8, 16, FF))


def expert_forward(rows, weight_gate, weight_up, weight_down):
    gate_act = jnp.dot(rows, weight_gate, preferred_element_type=jnp.float32)
    up_act = jnp.dot(rows, weight_up, preferred_element_type=jnp.float32)
    hidden = (jax.nn.silu(gate_act) * up_act).astype(jnp.bfloat16)
    output = lax.dot_general(
        hidden, weight_down, (((1,), (1,)), ((), ())), preferred_element_type=jnp.float32
    ).astype(jnp.bfloat16)
    return (gate_act, up_act, hidden, output)


def expert_backward(rows, upstream, weight_gate, weight_up, weight_down, gate_act, up_act, hidden):
    hidden_grad = jnp.dot(upstream, weight_down, preferred_element_type=jnp.float32)
    sigma = jax.nn.sigmoid(gate_act)
    gate_pre = (hidden_grad * up_act * sigma * (1.0 + gate_act * (1.0 - sigma))).astype(
        jnp.bfloat16
    )
    up_pre = (hidden_grad * gate_act * sigma).astype(jnp.bfloat16)
    contract = (((1,), (1,)), ((), ()))
    input_part = (
        lax.dot_general(gate_pre, weight_gate, contract, preferred_element_type=jnp.float32)
        + lax.dot_general(up_pre, weight_up, contract, preferred_element_type=jnp.float32)
    ).astype(jnp.bfloat16)
    over_rows = (((0,), (0,)), ((), ()))
    grad_gate = lax.dot_general(rows, gate_pre, over_rows, preferred_element_type=jnp.float32)
    grad_upper = lax.dot_general(rows, up_pre, over_rows, preferred_element_type=jnp.float32)
    grad_down = lax.dot_general(upstream, hidden, over_rows, preferred_element_type=jnp.float32)
    return (input_part, grad_gate, grad_upper, grad_down)


def per_device(tokens, expert_ids, gates, w_gate, w_up, w_down, cotangent):
    experts = lax.axis_size("expert")
    groups = lax.axis_size("dp")
    tok_rows = tokens.shape[0]
    capacity = (tok_rows * (TOPK - 1) + experts - 2) // (experts - 1)
    capacity = (capacity + ROW_TILE - 1) // ROW_TILE * ROW_TILE
    over_rows = (((0,), (0,)), ((), ()))
    highest = lax.Precision.HIGHEST
    expert_range = jnp.arange(experts, dtype=jnp.int32)
    matches = (expert_ids[:, :, None] == expert_range).astype(jnp.int32)
    counts = jnp.sum(matches, axis=(0, 1))
    hot_expert = jnp.argmax(counts)
    is_hot = expert_ids == hot_expert
    is_owner = lax.axis_index("expert") == hot_expert
    own_weights = (w_gate[0], w_up[0], w_down[0])

    piece = D // groups
    start = lax.axis_index("dp") * piece
    own_piece = jnp.stack(
        [lax.dynamic_slice_in_dim(weight, start, piece, 0) for weight in own_weights]
    )

    flat_matches = matches.reshape(tok_rows * TOPK, experts)
    before = jnp.cumsum(flat_matches, axis=0) - flat_matches
    position = jnp.sum(before * flat_matches, axis=1)
    target = jnp.where(is_hot.reshape(-1), -1, expert_ids.reshape(-1) * capacity + position)
    slot_ids = jnp.arange(experts * capacity, dtype=jnp.int32)
    dispatch_f = (slot_ids[:, None] == target[None, :]).astype(jnp.float32)
    per_token_f = jnp.sum(dispatch_f.reshape(experts * capacity, tok_rows, TOPK), axis=2)
    per_token = per_token_f.astype(jnp.bfloat16)
    slot_gate = jnp.dot(
        dispatch_f, gates.reshape(-1), precision=highest, preferred_element_type=jnp.float32
    )
    outgoing = jnp.dot(per_token, tokens, preferred_element_type=jnp.float32).astype(jnp.bfloat16)
    copied = jnp.dot(per_token, cotangent, preferred_element_type=jnp.float32)
    outgoing_grad = (slot_gate[:, None] * copied).astype(jnp.bfloat16)
    rows, incoming_grad, shadow_all = dispatch(
        hot_expert.astype(jnp.int32),
        outgoing.reshape(experts, capacity, D),
        outgoing_grad.reshape(experts, capacity, D),
        own_piece.reshape(3, 2, 8, 16, FF),
    )
    shadow_all = shadow_all.reshape(3, D, FF)
    shadow = (shadow_all[0], shadow_all[1], shadow_all[2])
    rows = rows.reshape(-1, D)
    incoming_grad = incoming_grad.reshape(-1, D)
    gate_act, up_act, hidden, expert_out = expert_forward(rows, *own_weights)
    input_rows, own_gate, own_upper, own_down = expert_backward(
        rows, incoming_grad, *own_weights, gate_act, up_act, hidden
    )
    hot_gate, hot_up, hot_hidden, hot_out = expert_forward(tokens, *shadow)
    upstream = cotangent.astype(jnp.float32)
    hot_weight = jnp.sum(jnp.where(is_hot, gates, 0.0), axis=1)
    hot_upstream = (hot_weight[:, None] * upstream).astype(jnp.bfloat16)
    hot_input, hot_gate_grad, hot_upper_grad, hot_down_grad = expert_backward(
        tokens, hot_upstream, *shadow, hot_gate, hot_up, hot_hidden
    )
    own_parts = jnp.stack([own_gate, own_upper, own_down]).astype(jnp.bfloat16)
    hot_parts = jnp.stack([hot_gate_grad, hot_upper_grad, hot_down_grad]).astype(jnp.bfloat16)
    returned, back_rows, own_sum, hot_total = combine(
        expert_out.reshape(experts, capacity, D),
        input_rows.reshape(experts, capacity, D),
        own_parts,
        hot_parts,
    )
    hot_total = hot_total.reshape(3, piece, FF).astype(jnp.float32)
    grads = own_sum + jnp.where(is_owner, hot_total, 0.0)
    returned_f = returned.reshape(-1, D).astype(jnp.float32)
    hot_out_f = hot_out.astype(jnp.float32)
    weighted = slot_gate[:, None] * returned_f
    mixed_cold = lax.dot_general(
        per_token_f, weighted, over_rows, precision=highest, preferred_element_type=jnp.float32
    )
    mixed = (mixed_cold + hot_weight[:, None] * hot_out_f).astype(jnp.bfloat16)
    slot_dot = jnp.sum(returned_f * copied, axis=1)
    cold_gates = jnp.dot(
        slot_dot, dispatch_f, precision=highest, preferred_element_type=jnp.float32
    ).reshape(tok_rows, TOPK)
    hot_dot = jnp.sum(upstream * hot_out_f, axis=1)
    gates_grad = cold_gates + jnp.where(is_hot, hot_dot[:, None], 0.0)
    cold_input = lax.dot_general(
        per_token, back_rows.reshape(-1, D), over_rows, preferred_element_type=jnp.float32
    )
    tokens_grad = (cold_input + hot_input.astype(jnp.float32)).astype(jnp.bfloat16)
    return (mixed, tokens_grad, gates_grad, grads[0][None], grads[1][None], grads[2][None])


def solution(mesh):
    return jax.shard_map(
        per_device,
        mesh=mesh,
        in_specs=(
            P(("dp", "expert"), None),
            P(("dp", "expert"), None),
            P(("dp", "expert"), None),
            P("expert", None, None),
            P("expert", None, None),
            P("expert", None, None),
            P(("dp", "expert"), None),
        ),
        out_specs=(
            P(("dp", "expert"), None),
            P(("dp", "expert"), None),
            P(("dp", "expert"), None),
            P("expert", "dp", None),
            P("expert", "dp", None),
            P("expert", "dp", None),
        ),
        check_vma=False,
    )
```
